256 devices in a mesh: feat: 16 (over x, y), layer: 4 (over z_lo), tok: 4 (over z_hi, core).
Axes of the slice: x: 4, y: 4, z: 8 (z_hi: 2, z_lo: 4; z = z_hi * 4 + z_lo), core: 2. Of those that a mesh axis runs over, the one named last changes fastest.
Arguments:
- captured: bfloat16 [4, 512, 2304], P('layer', 'tok', 'feat'), may hold values from -6 to 6
- target: bfloat16 [4, 512, 2304], P('layer', 'feat', 'tok'), may hold values from -6 to 6
- enc_weight: bfloat16 [4, 2304, 16384], P('layer', 'tok', 'feat'), may hold values from -0.125 to 0.125
- enc_bias: float32 [4, 16384], P('layer', 'feat'), may hold values from -3 to 3
- dec_weight: bfloat16 [4, 4, 16384, 2304], P('layer', None, 'feat', 'tok'), may hold values from -0.03125 to 0.03125
- dec_bias: float32 [4, 2304], P('layer', 'tok'), may hold values from -3 to 3
Outputs:
- enc_weight_grad: bfloat16 [4, 2304, 16384], P('layer', 'tok', 'feat')
- enc_bias_grad: float32 [4, 16384], P('layer', 'feat')
- dec_weight_grad: bfloat16 [4, 4, 16384, 2304], P('layer', None, 'feat', 'tok')
- dec_bias_grad: float32 [4, 2304], P('layer', 'tok')
The draws below stay inside these ranges and needn't reach their ends.
All inputs are finite; a program needn't handle non-finite values.
Results may differ from the reference program's by a relative error of at most 0.008.
Values may be sent and summed in bfloat16 or wider, within the bound.
No kernel may reach another device: no remote copies, remote signals or barrier semaphores. Data moves between devices by JAX's collectives and lax.ppermute only.
A program may use at most 64 MiB of HBM per device.

```python
import math
import jax
import jax.numpy as jnp
from jax import lax

D = 2304
N_LAY = 4
FEATURES = 16384
TOKENS = 512


def levels(stream_key, dims, shards, least, top_value):
    gain = 1.0
    for dim, blocks in shards:
        steps = jax.random.uniform(jax.random.fold_in(jax.random.fold_in(stream_key, 6), dim), (blocks,), jnp.float32, least / len(shards), top_value / len(shards))
        gain = gain * jnp.repeat(jnp.exp(steps), dims[dim] // blocks).reshape((-1,) + (1,) * (len(dims) - 1 - dim))
    return gain


def normal_values(stream_key, shape, deviation, most, cuts=(), held_as=jnp.bfloat16):
    level = levels(stream_key, shape, cuts, -0.22, 0.18) if cuts else 1.0
    values = jax.random.normal(stream_key, shape, jnp.float32) * deviation * level
    return jnp.minimum(jnp.maximum(values, -most), most).astype(held_as)


def setup_inputs(seed: int = 0) -> dict:
    seeds = jax.random.split(jax.random.key(seed), 7)
    captured = normal_values(seeds[0], (N_LAY, TOKENS, D), 1.0, 6.0, ((0, 4), (1, 4), (2, 16)))
    target = normal_values(seeds[1], (N_LAY, TOKENS, D), 1.0, 6.0, ((0, 4), (1, 16), (2, 4)))
    enc_weight = normal_values(seeds[2], (N_LAY, D, FEATURES), D ** -0.5, 0.125, ((0, 4), (1, 4), (2, 16)))
    enc_bias = normal_values(seeds[3], (N_LAY, FEATURES), 0.5, 3.0, ((0, 4), (1, 16)), jnp.float32)
    dec_weight = normal_values(seeds[4], (N_LAY, N_LAY, FEATURES, D), (FEATURES * 2) ** -0.5, 0.03125, ((0, 4), (2, 16), (3, 4)))
    dec_bias = normal_values(seeds[5], (N_LAY, D), 0.5, 3.0, ((0, 4), (1, 4)), jnp.float32)
    return {"captured": captured, "target": target, "enc_weight": enc_weight, "enc_bias": enc_bias, "dec_weight": dec_weight, "dec_bias": dec_bias}


def reference(captured, target, enc_weight, enc_bias, dec_weight, dec_bias):
    scale = 1.0 / math.sqrt(TOKENS)
    pres = []
    acts = []
    for layer in range(N_LAY):
        pre = jnp.dot(captured[layer], enc_weight[layer], preferred_element_type=jnp.float32) + enc_bias[layer]
        pres.append(pre)
        acts.append(jnp.maximum(pre, 0.0).astype(jnp.bfloat16))
    grads = []
    bias_rows = []
    for write in range(N_LAY):
        recon = jnp.zeros((TOKENS, D), jnp.float32)
        for layer in range(write + 1):
            recon = recon + jnp.dot(acts[layer], dec_weight[layer, write], preferred_element_type=jnp.float32)
        err = recon + dec_bias[write] - target[write].astype(jnp.float32)
        scaled = err * scale
        bias_rows.append(lax.optimization_barrier(jnp.sum(scaled, axis=0)))
        grads.append(scaled.astype(jnp.bfloat16))
    enc_grads = []
    enc_bias_rows = []
    dec_blocks = []
    for layer in range(N_LAY):
        grad_act = jnp.zeros((TOKENS, FEATURES), jnp.float32)
        row = []
        for write in range(N_LAY):
            if write < layer:
                row.append(jnp.zeros((FEATURES, D), jnp.bfloat16))
            else:
                row.append(jnp.dot(acts[layer].T, grads[write], preferred_element_type=jnp.float32).astype(jnp.bfloat16))
                grad_act = grad_act + jnp.dot(grads[write], dec_weight[layer, write].T, preferred_element_type=jnp.float32)
        dec_blocks.append(jnp.stack(row))
        grad_pre = jnp.where(pres[layer] > 0, grad_act, 0.0).astype(jnp.bfloat16)
        enc_bias_rows.append(lax.optimization_barrier(jnp.sum(grad_pre.astype(jnp.float32), axis=0)))
        enc_grads.append(jnp.dot(captured[layer].T, grad_pre, preferred_element_type=jnp.float32).astype(jnp.bfloat16))
    return (jnp.stack(enc_grads), jnp.stack(enc_bias_rows), jnp.stack(dec_blocks), jnp.stack(bias_rows))
```

```python
import math

import jax
import jax.numpy as jnp
from jax import lax
from jax.sharding import Mesh
from jax.sharding import PartitionSpec as P

FEAT = ("x", "y")
TOK = ("half", "core")


def swapped(value, axis):
    return lax.ppermute(value, axis, [(0, 1), (1, 0)])


def both(own, other, index, dim):
    first = jnp.where(index == 0, own, other)
    second = jnp.where(index == 0, other, own)
    return jnp.concatenate([first, second], axis=dim)


def sent_to_all(shard, axis):
    length = lax.axis_size(axis)
    return lax.all_to_all(
        jnp.broadcast_to(shard[None], (length, *shard.shape)), axis, 0, 0, tiled=True
    )


def dot(left, right, left_dim, right_dim):
    return lax.dot_general(
        left,
        right,
        (((left_dim,), (right_dim,)), ((), ())),
        preferred_element_type=jnp.float32,
    )


def on_device(captured, target, enc_weight, enc_bias, dec_weight, dec_bias):
    layer = lax.axis_index("layer")
    half = lax.axis_index("half")
    core = lax.axis_index("core")
    nlayer = dec_weight.shape[1]
    width = enc_weight.shape[1]
    feats = enc_weight.shape[2]
    rows = captured.shape[1]
    nfeat = lax.axis_size(FEAT)
    tokens = rows * lax.axis_size(TOK)
    scale = 1.0 / math.sqrt(tokens)
    encoder = enc_weight[0]
    decoder = dec_weight[0]

    cols = feats // 2
    mine = lax.dynamic_slice_in_dim(encoder, half * cols, cols, 1)
    theirs = lax.dynamic_slice_in_dim(encoder, (1 - half) * cols, cols, 1)
    crossed = swapped(theirs, "half")
    mine_next = swapped(mine, "core")
    small = captured[0].T
    small = both(small, swapped(small, "half"), half, 1)
    wide = sent_to_all(small, FEAT)
    wide = wide.reshape(-1, wide.shape[2])
    crossed_next = swapped(crossed, "core")

    def block(h, c):
        return lax.dynamic_slice_in_dim(wide, (h * 2 + c) * width, width, 0)

    pre = dot(block(half, core), mine, 0, 0)
    pre = pre + dot(block(half, 1 - core), mine_next, 0, 0)
    pre = pre + dot(block(1 - half, core), crossed, 0, 0)
    pre = pre + dot(block(1 - half, 1 - core), crossed_next, 0, 0)
    pre = pre + lax.dynamic_slice_in_dim(enc_bias, half * cols, cols, 1)
    act = jnp.maximum(pre, 0.0).astype(jnp.bfloat16)
    act = both(act, swapped(act, "half"), half, 1)
    pair = both(act[None], swapped(act, "core")[None], core, 0)
    act_all = pair.reshape(2, 2, rows, feats).swapaxes(0, 1).reshape(tokens, feats)

    moved = block(half, core)
    moved_next = swapped(block(half, 1 - core), "core")
    moved = both(moved[:, None], moved_next[:, None], core, 1)
    moved = moved.reshape(width, 2, 2, rows).swapaxes(1, 2).reshape(width, tokens)

    offset = dec_bias[0][None, :] - target[0].astype(jnp.float32)
    grads = [None] * nlayer
    for write in reversed(range(nlayer)):
        partial = dot(act_all, decoder[write], 1, 0).astype(jnp.bfloat16)
        partial = partial.reshape(nfeat, tokens // nfeat, width)
        pieces = lax.all_to_all(partial, FEAT, 0, 0, tiled=True)
        recon = jnp.sum(pieces.astype(jnp.float32), axis=0)
        recon = recon + jnp.where(layer == write, offset, 0.0)
        shared = recon.astype(jnp.bfloat16)
        for step in range(1, write + 1):
            ring = [(k, (k + step) % (write + 1)) for k in range(write + 1)]
            recon = recon + lax.ppermute(shared, "layer", ring).astype(jnp.float32)
        scaled = recon * scale
        grad = jnp.where(write >= layer, scaled, 0.0).astype(jnp.bfloat16)
        grads[write] = sent_to_all(grad, FEAT).reshape(tokens, width)

    dec_grads = jnp.zeros((nlayer, feats, width), jnp.bfloat16)
    grad_act = None
    for write in reversed(range(nlayer)):
        term = dot(grads[write], decoder[write], 1, 1)
        grad_act = term if grad_act is None else grad_act + term
    for write in reversed(range(nlayer)):
        block_grad = dot(act_all, grads[write], 0, 0).astype(jnp.bfloat16)
        dec_grads = lax.dynamic_update_index_in_dim(dec_grads, block_grad, write, 0)
    own = lax.dynamic_index_in_dim(jnp.stack(grads), layer, 0, keepdims=False)
    dec_bias_grad = jnp.sum(own.astype(jnp.float32), axis=0)

    few = tokens // 2
    keep = lax.dynamic_slice_in_dim(grad_act, core * few, few, 0)
    give = lax.dynamic_slice_in_dim(grad_act, (1 - core) * few, few, 0)
    keep = keep + swapped(give.astype(jnp.bfloat16), "core").astype(jnp.float32)
    keep = lax.optimization_barrier(keep.astype(jnp.bfloat16))
    grad_mine = keep.astype(jnp.float32) + swapped(keep, "half").astype(jnp.float32)
    act_mine = lax.dynamic_slice_in_dim(act_all, core * few, few, 0)
    grad_pre = jnp.where(act_mine > 0, grad_mine, 0.0).astype(jnp.bfloat16)
    grad_every = both(grad_pre, swapped(grad_pre, "core"), core, 0)
    enc_bias_grad = jnp.sum(grad_every.astype(jnp.float32), axis=0)
    enc_grad = dot(moved, grad_every, 1, 0).astype(jnp.bfloat16)
    return (enc_grad[None], enc_bias_grad[None], dec_grads[None], dec_bias_grad[None])


def solution(mesh):
    split = Mesh(
        mesh.devices.reshape(4, 4, mesh.shape["layer"], 2, 2),
        ("x", "y", "layer", "half", "core"),
    )
    return jax.shard_map(
        on_device,
        mesh=split,
        in_specs=(
            P("layer", TOK, FEAT),
            P("layer", FEAT, TOK),
            P("layer", TOK, FEAT),
            P("layer", FEAT),
            P("layer", None, FEAT, TOK),
            P("layer", TOK),
        ),
        out_specs=(
            P("layer", TOK, FEAT),
            P("layer", FEAT),
            P("layer", None, FEAT, TOK),
            P("layer", TOK),
        ),
        check_vma=False,
    )
```

```python
import functools
import itertools
import math

import jax
import jax.numpy as jnp
from jax import lax
from jax.experimental import pallas as pl
from jax.experimental.pallas import tpu as pltpu
from jax.sharding import Mesh
from jax.sharding import PartitionSpec as P


FEAT = ("x", "y")
TOK = ("half", "core")
ALL = ("x", "y", "layer", "half", "core")
RING = 4
GRANT = 14 * 2**20


def swapped(value, axis):
    return lax.ppermute(value, axis, [(0, 1), (1, 0)])


def both(own, other, index, dim):
    first = jnp.where(index == 0, own, other)
    second = jnp.where(index == 0, other, own)
    return jnp.concatenate([first, second], axis=dim)


def turned(value, step, first):
    sizes = [lax.axis_size(name) for name in ALL]
    pairs = []
    for place in itertools.product(*(range(size) for size in sizes)):
        dim = place[-1] if first else 1 - place[-1]
        there = list(place)
        there[dim] = (there[dim] + step) % sizes[dim]
        source, sink = 0, 0
        for size, here, far in zip(sizes, place, there):
            source, sink = source * size + here, sink * size + far
        pairs.append((source, sink))
    return lax.ppermute(value, ALL, pairs)


def gathered(value, together):
    around = jnp.stack([value] + [turned(value, k, False) for k in range(1, RING)])
    if together:
        corner = around[(0,) * (around.ndim - 2)][:16, :128]
        around, _ = lax.optimization_barrier((around, swapped(corner, "core")))
    return [around] + [turned(around, j, True) for j in range(1, RING)]


def dot(left, right, left_dim, right_dim):
    return lax.dot_general(
        left,
        right,
        (((left_dim,), (right_dim,)), ((), ())),
        preferred_element_type=jnp.float32,
    )


def in_place(core, first, second, far, near, pieces, where):
    for j in range(RING):
        for k in range(RING):
            one = lax.rem(first + far * j + RING, RING)
            two = lax.rem(second + near * k + RING, RING)
            x = jnp.where(core == 0, one, two)
            y = jnp.where(core == 0, two, one)
            where(x, y, pieces[j], k)


def widths_kernel(spot_ref, *refs):
    pieces, (out_ref, moved_ref, give_ref) = refs[:RING], refs[RING:]

    def put(x, y, piece, k):
        out_ref[x, y] = piece[k]

    in_place(spot_ref[0], spot_ref[1], spot_ref[2], -1, -1, pieces, put)
    moved_ref[...] = out_ref[spot_ref[4] * 2 + spot_ref[0]]
    give_ref[...] = out_ref[spot_ref[4] * 2 + 1 - spot_ref[0]]


def widths(spot, pieces):
    _, rows, tokens = pieces[0].shape
    whole = pl.BlockSpec(memory_space=pltpu.VMEM)
    return pl.pallas_call(
        widths_kernel,
        in_specs=[pl.BlockSpec(memory_space=pltpu.SMEM)] + [whole] * RING,
        out_specs=[whole] * 3,
        out_shape=[
            jax.ShapeDtypeStruct((RING, RING, rows, tokens), jnp.bfloat16),
            jax.ShapeDtypeStruct((RING, rows, tokens), jnp.bfloat16),
            jax.ShapeDtypeStruct((RING, rows, tokens), jnp.bfloat16),
        ],
        compiler_params=pltpu.CompilerParams(vmem_limit_bytes=GRANT),
        name="widths",
    )(spot, *pieces)


def encode_kernel(spot_ref, wide_ref, bias_ref, *refs):
    weights, out_ref = refs[:4], refs[4]
    core, half = spot_ref[0], spot_ref[4]
    places = (half * 2 + core, half * 2 + 1 - core, 2 - half * 2 + core, 3 - half * 2 - core)
    pre = jnp.where(half == 0, bias_ref[0], bias_ref[1])
    for place, weight_ref in zip(places, weights):
        pre = pre + dot(wide_ref[place], weight_ref[...], 0, 0)
    out_ref[...] = jnp.maximum(pre, 0.0).astype(jnp.bfloat16)


def encode(spot, wide, bias, weights):
    cols = weights[0].shape[1]
    whole = pl.BlockSpec(memory_space=pltpu.VMEM)
    return pl.pallas_call(
        encode_kernel,
        in_specs=[pl.BlockSpec(memory_space=pltpu.SMEM)] + [whole] * 6,
        out_specs=whole,
        out_shape=jax.ShapeDtypeStruct((wide.shape[2], cols), jnp.bfloat16),
        compiler_params=pltpu.CompilerParams(vmem_limit_bytes=GRANT),
        name="encode",
    )(spot, wide, bias, *weights)


def decode_kernel(step, spot_ref, mine_ref, other_ref, weight_ref, out_ref, rows):
    core = spot_ref[0]
    far = lax.rem(spot_ref[1] + step, RING)
    nlayer, part, width = out_ref.shape[1:]

    @pl.when(core == 0)
    def _():
        @pl.when(lax.rem(far, 2) == 0)
        def _():
            rows[...] = mine_ref[far // 2]

        @pl.when(lax.rem(far, 2) == 1)
        def _():
            rows[...] = other_ref[far // 2]

    @pl.when(core == 1)
    def _():
        for block in range(RING):
            act_ref = mine_ref if block % 2 else other_ref
            place = pl.ds(pl.multiple_of(far * part, part), part)
            rows[pl.ds(block * part, part), :] = act_ref[block // 2, place, :]

    for write in range(nlayer):
        output = dot(rows[...], weight_ref[write], 1, 1).astype(jnp.bfloat16)
        out_ref[:, write] = output.reshape(RING, part, width)


def decode(step, spot, mine, other, weight, part):
    few, feats = mine.shape
    nlayer, width, _ = weight.shape
    whole = pl.BlockSpec(memory_space=pltpu.VMEM)
    return pl.pallas_call(
        functools.partial(decode_kernel, step),
        in_specs=[pl.BlockSpec(memory_space=pltpu.SMEM)] + [whole] * 3,
        out_specs=whole,
        out_shape=jax.ShapeDtypeStruct((RING, nlayer, part, width), jnp.bfloat16),
        scratch_shapes=[pltpu.VMEM((RING * part, feats), jnp.bfloat16)],
        compiler_params=pltpu.CompilerParams(vmem_limit_bytes=GRANT),
    )(spot, mine.reshape(2, few // 2, feats), other.reshape(2, few // 2, feats), weight)


def halfway_kernel(spot_ref, bias_ref, target_ref, *refs):
    taken, outs = refs[:RING], refs[RING:]
    for k in range(RING):
        place = lax.rem(spot_ref[2] + k, RING)
        total = taken[0][place].astype(jnp.float32)
        for piece in taken[1:]:
            total = total + piece[place].astype(jnp.float32)
        outs[k][...] = total.astype(outs[k].dtype)
    outs[0][spot_ref[3]] += bias_ref[...] - target_ref[...].astype(jnp.float32)


def halfway(spot, bias, target, taken):
    shape = taken[0].shape[1:]
    whole = pl.BlockSpec(memory_space=pltpu.VMEM)
    return pl.pallas_call(
        halfway_kernel,
        in_specs=[pl.BlockSpec(memory_space=pltpu.SMEM)] + [whole] * (2 + RING),
        out_specs=[whole] * RING,
        out_shape=[jax.ShapeDtypeStruct(shape, jnp.float32)]
        + [jax.ShapeDtypeStruct(shape, jnp.bfloat16)] * (RING - 1),
        compiler_params=pltpu.CompilerParams(vmem_limit_bytes=GRANT),
        name="halfway",
    )(spot, bias, target, *taken)


def back_kernel(spot_ref, *refs):
    pieces, weight_ref = refs[:RING], refs[RING]
    grad_ref, keep_ref, give_ref, total = refs[RING + 1 :]
    step = pl.program_id(0)
    core = spot_ref[0]
    _, width = grad_ref.shape[-2:]

    def put(x, y, piece, k):
        grad_ref[0, x, y] = piece[k, 0]

    in_place(core, spot_ref[1], spot_ref[2], -1, -1, pieces, put)
    term = dot(grad_ref[0].reshape(-1, width), weight_ref[0], 1, 0)

    @pl.when(step == 0)
    def _():
        total[...] = term

    @pl.when(step > 0)
    def _():
        total[...] += term

    @pl.when(step == pl.num_programs(0) - 1)
    def _():
        rows = keep_ref.shape[0] // 2
        for half in range(2):
            place = pl.ds(half * rows, rows)
            first = pl.multiple_of((half * 2 + core) * rows, rows)
            keep_ref[place, :] = total[pl.ds(first, rows), :]
            first = pl.multiple_of((half * 2 + 1 - core) * rows, rows)
            give_ref[place, :] = total[pl.ds(first, rows), :].astype(jnp.bfloat16)


def back(spot, pieces, weight):
    _, nlayer, part, width = pieces[0].shape
    feats = weight.shape[2]
    few = RING * RING * part // 2
    return pl.pallas_call(
        back_kernel,
        grid_spec=pltpu.PrefetchScalarGridSpec(
            num_scalar_prefetch=1,
            grid=(nlayer,),
            in_specs=[pl.BlockSpec((RING, 1, part, width), lambda m, _: (0, m, 0, 0))] * RING
            + [pl.BlockSpec((1, width, feats), lambda m, _: (m, 0, 0))],
            out_specs=[
                pl.BlockSpec((1, RING, RING, part, width), lambda m, _: (m, 0, 0, 0, 0)),
                pl.BlockSpec((few, feats), lambda m, _: (0, 0)),
                pl.BlockSpec((few, feats), lambda m, _: (0, 0)),
            ],
            scratch_shapes=[pltpu.VMEM((2 * few, feats), jnp.float32)],
        ),
        out_shape=[
            jax.ShapeDtypeStruct((nlayer, RING, RING, part, width), jnp.bfloat16),
            jax.ShapeDtypeStruct((few, feats), jnp.float32),
            jax.ShapeDtypeStruct((few, feats), jnp.bfloat16),
        ],
        compiler_params=pltpu.CompilerParams(vmem_limit_bytes=GRANT),
        name="back",
    )(spot, *pieces, weight)


def outer_kernel(spot_ref, mine_ref, other_ref, grad_ref, out_ref, bias_ref):
    core = spot_ref[0]
    width = grad_ref.shape[-1]
    total = dot(grad_ref[0, :, core].reshape(-1, width), mine_ref[...], 0, 0)
    total += dot(grad_ref[0, :, 1 - core].reshape(-1, width), other_ref[...], 0, 0)
    out_ref[0] = total.astype(jnp.bfloat16)

    @pl.when(pl.program_id(0) == spot_ref[3])
    def _():
        grad = grad_ref[...].reshape(-1, width).astype(jnp.float32)
        bias_ref[...] = jnp.sum(grad, axis=0, keepdims=True)


def outer(spot, mine, other, grads):
    nlayer, _, _, part, width = grads.shape
    few, feats = mine.shape
    return pl.pallas_call(
        outer_kernel,
        grid_spec=pltpu.PrefetchScalarGridSpec(
            num_scalar_prefetch=1,
            grid=(nlayer,),
            in_specs=[
                pl.BlockSpec((few, feats), lambda m, _: (0, 0)),
                pl.BlockSpec((few, feats), lambda m, _: (0, 0)),
                pl.BlockSpec((1, 2, 2, RING, part, width), lambda m, _: (m, 0, 0, 0, 0, 0)),
            ],
            out_specs=[
                pl.BlockSpec((1, width, feats), lambda m, _: (m, 0, 0)),
                pl.BlockSpec((1, width), lambda m, _: (0, 0)),
            ],
        ),
        out_shape=[
            jax.ShapeDtypeStruct((nlayer, width, feats), jnp.bfloat16),
            jax.ShapeDtypeStruct((1, width), jnp.float32),
        ],
        compiler_params=pltpu.CompilerParams(vmem_limit_bytes=GRANT),
        cost_estimate=pl.CostEstimate(
            flops=4 * nlayer * few * feats * width,
            transcendentals=0,
            bytes_accessed=2 * nlayer * feats * width,
        ),
        name="outer",
    )(spot, mine, other, grads.reshape(nlayer, 2, 2, RING, part, width))


def last_kernel(moved_ref, next_ref, mine_ref, other_ref, out_ref, bias_ref):
    mine, other = mine_ref[...], other_ref[...]
    total = dot(moved_ref[...], mine, 1, 0) + dot(next_ref[...], other, 1, 0)
    out_ref[...] = total.astype(jnp.bfloat16)
    sums = [jnp.sum(g.astype(jnp.float32), axis=0, keepdims=True) for g in (mine, other)]
    bias_ref[...] = sums[0] + sums[1]


def last(moved, moved_next, mine, other):
    width, few = moved.shape
    feats = mine.shape[1]
    cut = min(feats, 256)
    return pl.pallas_call(
        last_kernel,
        grid=(feats // cut,),
        in_specs=[
            pl.BlockSpec((width, few), lambda n: (0, 0)),
            pl.BlockSpec((width, few), lambda n: (0, 0)),
            pl.BlockSpec((few, cut), lambda n: (0, n)),
            pl.BlockSpec((few, cut), lambda n: (0, n)),
        ],
        out_specs=[
            pl.BlockSpec((width, cut), lambda n: (0, n)),
            pl.BlockSpec((1, cut), lambda n: (0, n)),
        ],
        out_shape=[
            jax.ShapeDtypeStruct((width, feats), jnp.bfloat16),
            jax.ShapeDtypeStruct((1, feats), jnp.float32),
        ],
        compiler_params=pltpu.CompilerParams(vmem_limit_bytes=GRANT),
        name="last",
    )(moved, moved_next, mine, other)


def step(captured, target, enc_weight, enc_bias, dec_weight, dec_bias):
    layer = lax.axis_index("layer")
    half = lax.axis_index("half")
    core = lax.axis_index("core")
    nlayer = dec_weight.shape[1]
    width = enc_weight.shape[1]
    feats = enc_weight.shape[2]
    rows = captured.shape[1]
    tokens = rows * lax.axis_size(TOK)
    x, y = lax.axis_index("x"), lax.axis_index("y")
    first = jnp.where(core == 0, x, y)
    second = jnp.where(core == 0, y, x)
    spot = jnp.stack([core, first, second, layer, half])
    scale = 1.0 / math.sqrt(tokens)
    encoder = enc_weight[0]
    decoder = dec_weight[0].swapaxes(1, 2)

    cols = feats // 2
    theirs = lax.dynamic_slice_in_dim(encoder, (1 - half) * cols, cols, 1)
    theirs, captured, spot = lax.optimization_barrier((theirs, captured, spot))
    crossed = swapped(theirs, "half")
    small = captured[0].T
    small = both(small, swapped(small, "half"), half, 1)
    encoder, small = lax.optimization_barrier((encoder, small))
    mine = lax.dynamic_slice_in_dim(encoder, half * cols, cols, 1)
    mine_next = swapped(mine, "core")
    pieces = gathered(small, False)
    wide, moved, give = widths(spot, pieces)
    give, crossed = lax.optimization_barrier((give, crossed))
    crossed_next = swapped(crossed, "core")
    moved_next = swapped(give.reshape(width, -1), "core")
    crossed_next, moved_next = lax.optimization_barrier((crossed_next, moved_next))
    moved = moved.reshape(width, -1)
    act = encode(
        spot,
        wide.reshape(RING, width, -1),
        enc_bias.reshape(2, 1, cols),
        (mine, mine_next, crossed, crossed_next),
    )
    act = both(act, swapped(act, "half"), half, 1)
    act_next = swapped(act, "core")

    held = decoder
    taken = [None] * RING
    for j in (2, 1, 3, 0):
        part = decode(j, spot, act, act_next, held, target.shape[1])
        taken[j] = turned(part, j, True) if j else part
    parts = halfway(spot, dec_bias, target[0], taken)
    recon = parts[0]
    for k in range(1, RING):
        recon = recon + turned(parts[k], k, False).astype(jnp.float32)
    writes = lax.broadcasted_iota(jnp.int32, (nlayer, 1, 1), 0)
    recon = jnp.where(writes >= layer, recon, 0.0)
    shared = recon.astype(jnp.bfloat16)
    for far in range(1, nlayer):
        least = min(max(k, (k + far) % nlayer) for k in range(nlayer))
        ring = [(k, (k + far) % nlayer) for k in range(nlayer)]
        taken = lax.ppermute(shared[least:], "layer", ring).astype(jnp.float32)
        recon = recon + jnp.pad(taken, ((least, 0), (0, 0), (0, 0)))
    scaled = jnp.where(writes >= layer, recon * scale, 0.0)
    pieces = gathered(scaled.astype(jnp.bfloat16), True)

    grads, keep, give = back(spot, pieces, held)
    keep = keep + swapped(give, "core").astype(jnp.float32)
    keep = lax.optimization_barrier(keep.astype(jnp.bfloat16))
    crossing = swapped(keep, "half")
    grads, _ = lax.optimization_barrier((grads, keep))
    dec_grads, dec_bias_grad = outer(spot, act, act_next, grads)
    grad_mine = keep.astype(jnp.float32) + crossing.astype(jnp.float32)
    grad_pre = jnp.where(act > 0, grad_mine, 0.0).astype(jnp.bfloat16)
    enc_grad, enc_bias_grad = last(moved, moved_next, grad_pre, swapped(grad_pre, "core"))
    return (enc_grad[None], enc_bias_grad, dec_grads.swapaxes(1, 2)[None], dec_bias_grad)


def solution(mesh):
    split = Mesh(
        mesh.devices.reshape(4, 4, mesh.shape["layer"], 2, 2),
        ("x", "y", "layer", "half", "core"),
    )
    return jax.shard_map(
        step,
        mesh=split,
        in_specs=(
            P("layer", TOK, FEAT),
            P("layer", FEAT, TOK),
            P("layer", TOK, FEAT),
            P("layer", FEAT),
            P("layer", None, FEAT, TOK),
            P("layer", TOK),
        ),
        out_specs=(
            P("layer", TOK, FEAT),
            P("layer", FEAT),
            P("layer", None, FEAT, TOK),
            P("layer", TOK),
        ),
        check_vma=False,
    )
```

```python
import functools
import itertools
import math

import jax
import jax.numpy as jnp
from jax import lax
from jax.experimental import pallas as pl
from jax.experimental.pallas import tpu as pltpu
from jax.sharding import Mesh
from jax.sharding import PartitionSpec as P


FEAT = ("x", "y")
TOK = ("half", "core")
ALL = ("x", "y", "layer", "half", "core")
RING = 4
GRANT = 14 * 2**20


def swapped(value, axis):
    return lax.ppermute(value, axis, [(0, 1), (1, 0)])


def both(own, other, index, dim):
    first = jnp.where(index == 0, own, other)
    second = jnp.where(index == 0, other, own)
    return jnp.concatenate([first, second], axis=dim)


def turned(value, step, first):
    sizes = [lax.axis_size(name) for name in ALL]
    pairs = []
    for place in itertools.product(*(range(size) for size in sizes)):
        dim = place[-1] if first else 1 - place[-1]
        there = list(place)
        there[dim] = (there[dim] + step) % sizes[dim]
        source, sink = 0, 0
        for size, here, far in zip(sizes, place, there):
            source, sink = source * size + here, sink * size + far
        pairs.append((source, sink))
    return lax.ppermute(value, ALL, pairs)


def gathered(value):
    around = jnp.stack([value] + [turned(value, k, False) for k in range(1, RING)])
    return [around] + [turned(around, j, True) for j in range(1, RING)]


def forwarded(value):
    around = jnp.stack([value] + [turned(value, k, False) for k in range(1, RING)])
    corner = around[(0,) * (around.ndim - 2)][:16, :128]
    around, _ = lax.optimization_barrier((around, swapped(corner, "core")))
    before, after = turned(around, 1, True), turned(around, RING - 1, True)
    low = turned(before[: RING // 2], 1, True)
    high = turned(after[RING // 2 :], RING - 1, True)
    return around, before, (low, high), after


def dot(left, right, left_dim, right_dim):
    return lax.dot_general(
        left,
        right,
        (((left_dim,), (right_dim,)), ((), ())),
        preferred_element_type=jnp.float32,
    )


def in_place(core, first, second, far, near, pieces, where):
    for j in range(RING):
        for k in range(RING):
            one = lax.rem(first + far * j + RING, RING)
            two = lax.rem(second + near * k + RING, RING)
            x = jnp.where(core == 0, one, two)
            y = jnp.where(core == 0, two, one)
            where(x, y, pieces[j], k)


def widths_kernel(spot_ref, *refs):
    pieces, (out_ref, moved_ref, give_ref) = refs[:RING], refs[RING:]

    def put(x, y, piece, k):
        out_ref[x, y] = piece[k]

    in_place(spot_ref[0], spot_ref[1], spot_ref[2], -1, -1, pieces, put)
    moved_ref[...] = out_ref[spot_ref[4] * 2 + spot_ref[0]]
    give_ref[...] = out_ref[spot_ref[4] * 2 + 1 - spot_ref[0]]


def widths(spot, pieces):
    _, rows, tokens = pieces[0].shape
    whole = pl.BlockSpec(memory_space=pltpu.VMEM)
    return pl.pallas_call(
        widths_kernel,
        in_specs=[pl.BlockSpec(memory_space=pltpu.SMEM)] + [whole] * RING,
        out_specs=[whole] * 3,
        out_shape=[
            jax.ShapeDtypeStruct((RING, RING, rows, tokens), jnp.bfloat16),
            jax.ShapeDtypeStruct((RING, rows, tokens), jnp.bfloat16),
            jax.ShapeDtypeStruct((RING, rows, tokens), jnp.bfloat16),
        ],
        compiler_params=pltpu.CompilerParams(vmem_limit_bytes=GRANT),
        name="widths",
    )(spot, *pieces)


def encode_kernel(spot_ref, wide_ref, bias_ref, *refs):
    weights, out_ref = refs[:4], refs[4]
    core, half = spot_ref[0], spot_ref[4]
    places = (half * 2 + core, half * 2 + 1 - core, 2 - half * 2 + core, 3 - half * 2 - core)
    pre = jnp.where(half == 0, bias_ref[0], bias_ref[1])
    for place, weight_ref in zip(places, weights):
        pre = pre + dot(wide_ref[place], weight_ref[...], 0, 0)
    out_ref[...] = jnp.maximum(pre, 0.0).astype(jnp.bfloat16)


def encode(spot, wide, bias, weights):
    cols = weights[0].shape[1]
    whole = pl.BlockSpec(memory_space=pltpu.VMEM)
    return pl.pallas_call(
        encode_kernel,
        in_specs=[pl.BlockSpec(memory_space=pltpu.SMEM)] + [whole] * 6,
        out_specs=whole,
        out_shape=jax.ShapeDtypeStruct((wide.shape[2], cols), jnp.bfloat16),
        compiler_params=pltpu.CompilerParams(vmem_limit_bytes=GRANT),
        name="encode",
    )(spot, wide, bias, *weights)


def decode_kernel(step, spot_ref, mine_ref, other_ref, weight_ref, out_ref, rows):
    core = spot_ref[0]
    far = lax.rem(spot_ref[1] + step, RING)
    nlayer, part, width = out_ref.shape[1:]

    @pl.when(core == 0)
    def _():
        @pl.when(lax.rem(far, 2) == 0)
        def _():
            rows[...] = mine_ref[far // 2]

        @pl.when(lax.rem(far, 2) == 1)
        def _():
            rows[...] = other_ref[far // 2]

    @pl.when(core == 1)
    def _():
        for block in range(RING):
            act_ref = mine_ref if block % 2 else other_ref
            place = pl.ds(pl.multiple_of(far * part, part), part)
            rows[pl.ds(block * part, part), :] = act_ref[block // 2, place, :]

    for write in range(nlayer):
        output = dot(rows[...], weight_ref[write], 1, 1).astype(jnp.bfloat16)
        out_ref[:, write] = output.reshape(RING, part, width)


def decode(step, spot, mine, other, weight, part):
    few, feats = mine.shape
    nlayer, width, _ = weight.shape
    whole = pl.BlockSpec(memory_space=pltpu.VMEM)
    return pl.pallas_call(
        functools.partial(decode_kernel, step),
        in_specs=[pl.BlockSpec(memory_space=pltpu.SMEM)] + [whole] * 3,
        out_specs=whole,
        out_shape=jax.ShapeDtypeStruct((RING, nlayer, part, width), jnp.bfloat16),
        scratch_shapes=[pltpu.VMEM((RING * part, feats), jnp.bfloat16)],
        compiler_params=pltpu.CompilerParams(vmem_limit_bytes=GRANT),
    )(spot, mine.reshape(2, few // 2, feats), other.reshape(2, few // 2, feats), weight)


def halfway_kernel(spot_ref, bias_ref, target_ref, *refs):
    taken, outs = refs[:RING], refs[RING:]
    for k in range(RING):
        place = lax.rem(spot_ref[2] + k, RING)
        total = taken[0][place].astype(jnp.float32)
        for piece in taken[1:]:
            total = total + piece[place].astype(jnp.float32)
        outs[k][...] = total.astype(outs[k].dtype)
    outs[0][spot_ref[3]] += bias_ref[...] - target_ref[...].astype(jnp.float32)


def halfway(spot, bias, target, taken):
    shape = taken[0].shape[1:]
    whole = pl.BlockSpec(memory_space=pltpu.VMEM)
    return pl.pallas_call(
        halfway_kernel,
        in_specs=[pl.BlockSpec(memory_space=pltpu.SMEM)] + [whole] * (2 + RING),
        out_specs=[whole] * RING,
        out_shape=[jax.ShapeDtypeStruct(shape, jnp.float32)]
        + [jax.ShapeDtypeStruct(shape, jnp.bfloat16)] * (RING - 1),
        compiler_params=pltpu.CompilerParams(vmem_limit_bytes=GRANT),
        name="halfway",
    )(spot, bias, target, *taken)


def rows_of(piece, write):
    value = piece[:, write]
    return value.reshape(-1, value.shape[-1])


def near_kernel(*refs):
    pieces, weight_ref, out_ref = refs[:-2], refs[-2], refs[-1]
    for write in range(weight_ref.shape[0]):
        grad = jnp.concatenate([rows_of(piece, write) for piece in pieces], axis=0)
        term = dot(grad, weight_ref[write], 1, 0)
        if write == 0:
            out_ref[...] = term
        else:
            out_ref[...] += term


def near_rows(pieces, weight):
    rows = len(pieces) * RING * pieces[0].shape[2]
    whole = pl.BlockSpec(memory_space=pltpu.VMEM)
    return pl.pallas_call(
        near_kernel,
        in_specs=[whole] * (len(pieces) + 1),
        out_specs=whole,
        out_shape=jax.ShapeDtypeStruct((rows, weight.shape[2]), jnp.float32),
        compiler_params=pltpu.CompilerParams(vmem_limit_bytes=GRANT),
        name="near",
    )(*pieces, weight)


def back_kernel(spot_ref, low_ref, high_ref, weight_ref, near_ref, keep_ref, give_ref, total):
    core = spot_ref[0]
    part = keep_ref.shape[2]
    for write in range(weight_ref.shape[0]):
        grad = jnp.concatenate([rows_of(low_ref, write), rows_of(high_ref, write)], axis=0)
        term = dot(grad, weight_ref[write], 1, 0)
        if write == 0:
            total[...] = term
        else:
            total[...] += term

    def put(x, y, source, k):
        ref, first = source
        rows = ref[pl.ds(first + k * part, part), :]

        @pl.when(lax.rem(x, 2) == core)
        def _():
            keep_ref[x // 2, y] = rows

        @pl.when(lax.rem(x, 2) != core)
        def _():
            give_ref[x // 2, y] = rows.astype(jnp.bfloat16)

    block = RING * part
    sources = ((near_ref, 0), (near_ref, block), (total, 0), (near_ref, 2 * block))
    in_place(core, spot_ref[1], spot_ref[2], -1, -1, sources, put)


def back(spot, far, weight, near):
    low, high = far
    part = low.shape[2]
    feats = weight.shape[2]
    shape = (2, RING, part, feats)
    whole = pl.BlockSpec(memory_space=pltpu.VMEM)
    keep, give = pl.pallas_call(
        back_kernel,
        in_specs=[pl.BlockSpec(memory_space=pltpu.SMEM)] + [whole] * 4,
        out_specs=[whole] * 2,
        out_shape=[
            jax.ShapeDtypeStruct(shape, jnp.float32),
            jax.ShapeDtypeStruct(shape, jnp.bfloat16),
        ],
        scratch_shapes=[pltpu.VMEM((RING * part, feats), jnp.float32)],
        compiler_params=pltpu.CompilerParams(vmem_limit_bytes=GRANT),
        name="back",
    )(spot, low, high, weight, near)
    return keep.reshape(-1, feats), give.reshape(-1, feats)


def outer_kernel(spot_ref, mine_ref, other_ref, *refs):
    around, before, low, high, after, out_ref, bias_ref, held = refs
    core = spot_ref[0]
    width = held.shape[-1]
    cut = low.shape[0]

    def put(x, y, piece, k):
        if piece is None:
            held[x // 2, lax.rem(x, 2), y] = low[k, 0] if k < cut else high[k - cut, 0]
        else:
            held[x // 2, lax.rem(x, 2), y] = piece[k, 0]

    in_place(core, spot_ref[1], spot_ref[2], -1, -1, (around, before, None, after), put)
    total = dot(held[:, core].reshape(-1, width), mine_ref[...], 0, 0)
    total += dot(held[:, 1 - core].reshape(-1, width), other_ref[...], 0, 0)
    out_ref[0] = total.astype(jnp.bfloat16)

    @pl.when(pl.program_id(0) == spot_ref[3])
    def _():
        grad = held[...].reshape(-1, width).astype(jnp.float32)
        bias_ref[...] = jnp.sum(grad, axis=0, keepdims=True)


def outer(spot, mine, other, pieces):
    _, nlayer, part, width = pieces[0].shape
    few, feats = mine.shape
    return pl.pallas_call(
        outer_kernel,
        grid_spec=pltpu.PrefetchScalarGridSpec(
            num_scalar_prefetch=1,
            grid=(nlayer,),
            in_specs=[
                pl.BlockSpec((few, feats), lambda m, _: (0, 0)),
                pl.BlockSpec((few, feats), lambda m, _: (0, 0)),
            ]
            + [
                pl.BlockSpec((piece.shape[0], 1, part, width), lambda m, _: (0, m, 0, 0))
                for piece in pieces
            ],
            out_specs=[
                pl.BlockSpec((1, width, feats), lambda m, _: (m, 0, 0)),
                pl.BlockSpec((1, width), lambda m, _: (0, 0)),
            ],
            scratch_shapes=[pltpu.VMEM((2, 2, RING, part, width), jnp.bfloat16)],
        ),
        out_shape=[
            jax.ShapeDtypeStruct((nlayer, width, feats), jnp.bfloat16),
            jax.ShapeDtypeStruct((1, width), jnp.float32),
        ],
        compiler_params=pltpu.CompilerParams(vmem_limit_bytes=GRANT),
        cost_estimate=pl.CostEstimate(
            flops=4 * nlayer * few * feats * width,
            transcendentals=0,
            bytes_accessed=2 * nlayer * feats * width,
        ),
        name="outer",
    )(spot, mine, other, *pieces)


def last_kernel(moved_ref, next_ref, mine_ref, other_ref, out_ref, bias_ref):
    mine, other = mine_ref[...], other_ref[...]
    total = dot(moved_ref[...], mine, 1, 0) + dot(next_ref[...], other, 1, 0)
    out_ref[...] = total.astype(jnp.bfloat16)
    sums = [jnp.sum(g.astype(jnp.float32), axis=0, keepdims=True) for g in (mine, other)]
    bias_ref[...] = sums[0] + sums[1]


def last(moved, moved_next, mine, other):
    width, few = moved.shape
    feats = mine.shape[1]
    cut = min(feats, 256)
    return pl.pallas_call(
        last_kernel,
        grid=(feats // cut,),
        in_specs=[
            pl.BlockSpec((width, few), lambda n: (0, 0)),
            pl.BlockSpec((width, few), lambda n: (0, 0)),
            pl.BlockSpec((few, cut), lambda n: (0, n)),
            pl.BlockSpec((few, cut), lambda n: (0, n)),
        ],
        out_specs=[
            pl.BlockSpec((width, cut), lambda n: (0, n)),
            pl.BlockSpec((1, cut), lambda n: (0, n)),
        ],
        out_shape=[
            jax.ShapeDtypeStruct((width, feats), jnp.bfloat16),
            jax.ShapeDtypeStruct((1, feats), jnp.float32),
        ],
        compiler_params=pltpu.CompilerParams(vmem_limit_bytes=GRANT),
        name="last",
    )(moved, moved_next, mine, other)


def step(captured, target, enc_weight, enc_bias, dec_weight, dec_bias):
    layer = lax.axis_index("layer")
    half = lax.axis_index("half")
    core = lax.axis_index("core")
    nlayer = dec_weight.shape[1]
    width = enc_weight.shape[1]
    feats = enc_weight.shape[2]
    rows = captured.shape[1]
    tokens = rows * lax.axis_size(TOK)
    x, y = lax.axis_index("x"), lax.axis_index("y")
    first = jnp.where(core == 0, x, y)
    second = jnp.where(core == 0, y, x)
    spot = jnp.stack([core, first, second, layer, half])
    scale = 1.0 / math.sqrt(tokens)
    encoder = enc_weight[0]
    decoder = dec_weight[0].swapaxes(1, 2)

    cols = feats // 2
    theirs = lax.dynamic_slice_in_dim(encoder, (1 - half) * cols, cols, 1)
    theirs, captured, spot = lax.optimization_barrier((theirs, captured, spot))
    crossed = swapped(theirs, "half")
    small = captured[0].T
    small = both(small, swapped(small, "half"), half, 1)
    encoder, small = lax.optimization_barrier((encoder, small))
    mine = lax.dynamic_slice_in_dim(encoder, half * cols, cols, 1)
    mine_next = swapped(mine, "core")
    pieces = gathered(small)
    wide, moved, give = widths(spot, pieces)
    give, crossed = lax.optimization_barrier((give, crossed))
    crossed_next = swapped(crossed, "core")
    moved_next = swapped(give.reshape(width, -1), "core")
    crossed_next, moved_next = lax.optimization_barrier((crossed_next, moved_next))
    moved = moved.reshape(width, -1)
    act = encode(
        spot,
        wide.reshape(RING, width, -1),
        enc_bias.reshape(2, 1, cols),
        (mine, mine_next, crossed, crossed_next),
    )
    act = both(act, swapped(act, "half"), half, 1)
    act_next = swapped(act, "core")

    held = decoder
    taken = [None] * RING
    for j in (2, 1, 3, 0):
        part = decode(j, spot, act, act_next, held, target.shape[1])
        taken[j] = turned(part, j, True) if j else part
    parts = halfway(spot, dec_bias, target[0], taken)
    recon = parts[0]
    for k in range(1, RING):
        recon = recon + turned(parts[k], k, False).astype(jnp.float32)
    writes = lax.broadcasted_iota(jnp.int32, (nlayer, 1, 1), 0)
    recon = jnp.where(writes >= layer, recon, 0.0)
    shared = recon.astype(jnp.bfloat16)
    for far in range(1, nlayer):
        least = min(max(k, (k + far) % nlayer) for k in range(nlayer))
        ring = [(k, (k + far) % nlayer) for k in range(nlayer)]
        taken = lax.ppermute(shared[least:], "layer", ring).astype(jnp.float32)
        recon = recon + jnp.pad(taken, ((least, 0), (0, 0), (0, 0)))
    scaled = jnp.where(writes >= layer, recon * scale, 0.0)
    around, before, far, after = forwarded(scaled.astype(jnp.bfloat16))

    near = near_rows((around, before, after), held)
    keep, give = back(spot, far, held, near)
    keep = keep + swapped(give, "core").astype(jnp.float32)
    keep = lax.optimization_barrier(keep.astype(jnp.bfloat16))
    crossing = swapped(keep, "half")
    grads, _ = lax.optimization_barrier(((around, before, *far, after), keep))
    dec_grads, dec_bias_grad = outer(spot, act, act_next, grads)
    grad_mine = keep.astype(jnp.float32) + crossing.astype(jnp.float32)
    grad_pre = jnp.where(act > 0, grad_mine, 0.0).astype(jnp.bfloat16)
    enc_grad, enc_bias_grad = last(moved, moved_next, grad_pre, swapped(grad_pre, "core"))
    return (enc_grad[None], enc_bias_grad, dec_grads.swapaxes(1, 2)[None], dec_bias_grad)


def solution(mesh):
    split = Mesh(
        mesh.devices.reshape(4, 4, mesh.shape["layer"], 2, 2),
        ("x", "y", "layer", "half", "core"),
    )
    return jax.shard_map(
        step,
        mesh=split,
        in_specs=(
            P("layer", TOK, FEAT),
            P("layer", FEAT, TOK),
            P("layer", TOK, FEAT),
            P("layer", FEAT),
            P("layer", None, FEAT, TOK),
            P("layer", TOK),
        ),
        out_specs=(
            P("layer", TOK, FEAT),
            P("layer", FEAT),
            P("layer", None, FEAT, TOK),
            P("layer", TOK),
        ),
        check_vma=False,
    )
```

```python
import functools
import itertools
import math

import jax
import jax.numpy as jnp
from jax import lax
from jax.experimental import pallas as pl
from jax.experimental.pallas import tpu as pltpu
from jax.sharding import Mesh
from jax.sharding import PartitionSpec as P


FEAT = ("x", "y")
TOK = ("half", "core")
ALL = ("x", "y", "layer", "half", "core")
RING = 4
GRANT = 14 * 2**20


def swapped(value, axis):
    return lax.ppermute(value, axis, [(0, 1), (1, 0)])


def both(own, other, index, dim):
    first = jnp.where(index == 0, own, other)
    second = jnp.where(index == 0, other, own)
    return jnp.concatenate([first, second], axis=dim)


def turned(value, step, first):
    sizes = [lax.axis_size(name) for name in ALL]
    pairs = []
    for place in itertools.product(*(range(size) for size in sizes)):
        dim = place[-1] if first else 1 - place[-1]
        there = list(place)
        there[dim] = (there[dim] + step) % sizes[dim]
        source, sink = 0, 0
        for size, here, far in zip(sizes, place, there):
            source, sink = source * size + here, sink * size + far
        pairs.append((source, sink))
    return lax.ppermute(value, ALL, pairs)


def gathered(value):
    around = jnp.stack([value] + [turned(value, k, False) for k in range(1, RING)])
    return [around] + [turned(around, j, True) for j in range(1, RING)]


def forwarded(value):
    around = jnp.stack([value] + [turned(value, k, False) for k in range(1, RING)])
    corner = around[(0,) * (around.ndim - 2)][:16, :128]
    around, _ = lax.optimization_barrier((around, swapped(corner, "core")))
    before, after = turned(around, 1, True), turned(around, RING - 1, True)
    low = turned(before[: RING // 2], 1, True)
    high = turned(after[RING // 2 :], RING - 1, True)
    return around, before, (low, high), after


def dot(left, right, left_dim, right_dim):
    return lax.dot_general(
        left,
        right,
        (((left_dim,), (right_dim,)), ((), ())),
        preferred_element_type=jnp.float32,
    )


def in_place(core, first, second, far, near, pieces, where):
    for j in range(RING):
        for k in range(RING):
            one = lax.rem(first + far * j + RING, RING)
            two = lax.rem(second + near * k + RING, RING)
            x = jnp.where(core == 0, one, two)
            y = jnp.where(core == 0, two, one)
            where(x, y, pieces[j], k)


def widths_kernel(spot_ref, *refs):
    pieces, (out_ref, moved_ref, give_ref) = refs[:RING], refs[RING:]

    def put(x, y, piece, k):
        out_ref[x, y] = piece[k]

    in_place(spot_ref[0], spot_ref[1], spot_ref[2], -1, -1, pieces, put)
    moved_ref[...] = out_ref[spot_ref[4] * 2 + spot_ref[0]]
    give_ref[...] = out_ref[spot_ref[4] * 2 + 1 - spot_ref[0]]


def widths(spot, pieces):
    _, rows, tokens = pieces[0].shape
    whole = pl.BlockSpec(memory_space=pltpu.VMEM)
    return pl.pallas_call(
        widths_kernel,
        in_specs=[pl.BlockSpec(memory_space=pltpu.SMEM)] + [whole] * RING,
        out_specs=[whole] * 3,
        out_shape=[
            jax.ShapeDtypeStruct((RING, RING, rows, tokens), jnp.bfloat16),
            jax.ShapeDtypeStruct((RING, rows, tokens), jnp.bfloat16),
            jax.ShapeDtypeStruct((RING, rows, tokens), jnp.bfloat16),
        ],
        compiler_params=pltpu.CompilerParams(vmem_limit_bytes=GRANT),
        name="widths",
    )(spot, *pieces)


def encode_kernel(spot_ref, wide_ref, bias_ref, *refs):
    weights, out_ref = refs[:4], refs[4]
    core, half = spot_ref[0], spot_ref[4]
    places = (half * 2 + core, half * 2 + 1 - core, 2 - half * 2 + core, 3 - half * 2 - core)
    pre = jnp.where(half == 0, bias_ref[0], bias_ref[1])
    for place, weight_ref in zip(places, weights):
        pre = pre + dot(wide_ref[place], weight_ref[...], 0, 0)
    out_ref[...] = jnp.maximum(pre, 0.0).astype(jnp.bfloat16)


def encode(spot, wide, bias, weights):
    cols = weights[0].shape[1]
    whole = pl.BlockSpec(memory_space=pltpu.VMEM)
    return pl.pallas_call(
        encode_kernel,
        in_specs=[pl.BlockSpec(memory_space=pltpu.SMEM)] + [whole] * 6,
        out_specs=whole,
        out_shape=jax.ShapeDtypeStruct((wide.shape[2], cols), jnp.bfloat16),
        compiler_params=pltpu.CompilerParams(vmem_limit_bytes=GRANT),
        name="encode",
    )(spot, wide, bias, *weights)


def decode_kernel(steps, spot_ref, mine_ref, other_ref, weight_ref, *refs):
    outs, rows = refs[:-1], refs[-1]
    core = spot_ref[0]
    nlayer, part, width = outs[0].shape[1:]
    block = RING * part
    for index, step in enumerate(steps):
        far = lax.rem(spot_ref[1] + step, RING)
        first = index * block

        @pl.when(core == 0)
        def _():
            @pl.when(lax.rem(far, 2) == 0)
            def _():
                rows[pl.ds(first, block), :] = mine_ref[far // 2]

            @pl.when(lax.rem(far, 2) == 1)
            def _():
                rows[pl.ds(first, block), :] = other_ref[far // 2]

        @pl.when(core == 1)
        def _():
            for t in range(RING):
                act_ref = mine_ref if t % 2 else other_ref
                place = pl.ds(pl.multiple_of(far * part, part), part)
                rows[pl.ds(first + t * part, part), :] = act_ref[t // 2, place, :]

    for write in range(nlayer):
        output = dot(rows[...], weight_ref[write], 1, 1).astype(jnp.bfloat16)
        for index, out_ref in enumerate(outs):
            piece = output[index * block : (index + 1) * block]
            out_ref[:, write] = piece.reshape(RING, part, width)


def decode(steps, spot, mine, other, weight, part):
    few, feats = mine.shape
    nlayer, width, _ = weight.shape
    whole = pl.BlockSpec(memory_space=pltpu.VMEM)
    return pl.pallas_call(
        functools.partial(decode_kernel, steps),
        in_specs=[pl.BlockSpec(memory_space=pltpu.SMEM)] + [whole] * 3,
        out_specs=[whole] * len(steps),
        out_shape=[jax.ShapeDtypeStruct((RING, nlayer, part, width), jnp.bfloat16)] * len(steps),
        scratch_shapes=[pltpu.VMEM((len(steps) * RING * part, feats), jnp.bfloat16)],
        compiler_params=pltpu.CompilerParams(vmem_limit_bytes=GRANT),
    )(spot, mine.reshape(2, few // 2, feats), other.reshape(2, few // 2, feats), weight)


def halfway_kernel(spot_ref, bias_ref, target_ref, *refs):
    taken, outs = refs[:RING], refs[RING:]
    for k in range(RING):
        place = lax.rem(spot_ref[2] + k, RING)
        total = taken[0][place].astype(jnp.float32)
        for piece in taken[1:]:
            total = total + piece[place].astype(jnp.float32)
        outs[k][...] = total.astype(outs[k].dtype)
    outs[0][spot_ref[3]] += bias_ref[...] - target_ref[...].astype(jnp.float32)


def halfway(spot, bias, target, taken):
    shape = taken[0].shape[1:]
    whole = pl.BlockSpec(memory_space=pltpu.VMEM)
    return pl.pallas_call(
        halfway_kernel,
        in_specs=[pl.BlockSpec(memory_space=pltpu.SMEM)] + [whole] * (2 + RING),
        out_specs=[whole] * RING,
        out_shape=[jax.ShapeDtypeStruct(shape, jnp.float32)]
        + [jax.ShapeDtypeStruct(shape, jnp.bfloat16)] * (RING - 1),
        compiler_params=pltpu.CompilerParams(vmem_limit_bytes=GRANT),
        name="halfway",
    )(spot, bias, target, *taken)


def rows_of(piece, write):
    value = piece[:, write]
    return value.reshape(-1, value.shape[-1])


def near_kernel(*refs):
    pieces, weight_ref, out_ref = refs[:-2], refs[-2], refs[-1]
    for write in range(weight_ref.shape[0]):
        grad = jnp.concatenate([rows_of(piece, write) for piece in pieces], axis=0)
        term = dot(grad, weight_ref[write], 1, 0)
        if write == 0:
            out_ref[...] = term
        else:
            out_ref[...] += term


def near_rows(pieces, weight):
    rows = len(pieces) * RING * pieces[0].shape[2]
    whole = pl.BlockSpec(memory_space=pltpu.VMEM)
    return pl.pallas_call(
        near_kernel,
        in_specs=[whole] * (len(pieces) + 1),
        out_specs=whole,
        out_shape=jax.ShapeDtypeStruct((rows, weight.shape[2]), jnp.float32),
        compiler_params=pltpu.CompilerParams(vmem_limit_bytes=GRANT),
        name="near",
    )(*pieces, weight)


def back_kernel(spot_ref, low_ref, high_ref, weight_ref, near_ref, *refs):
    keeps, gives, total = refs[:2], refs[2:4], refs[4]
    core = spot_ref[0]
    part, cols = keeps[0].shape[2:]
    for write in range(weight_ref.shape[0]):
        grad = jnp.concatenate([rows_of(low_ref, write), rows_of(high_ref, write)], axis=0)
        term = dot(grad, weight_ref[write], 1, 0)
        if write == 0:
            total[...] = term
        else:
            total[...] += term

    def put(x, y, source, k):
        ref, first = source
        rows = ref[pl.ds(first + k * part, part), :]

        @pl.when(lax.rem(x, 2) == core)
        def _():
            for side in range(2):
                keeps[side][x // 2, y] = rows[:, side * cols : (side + 1) * cols]

        @pl.when(lax.rem(x, 2) != core)
        def _():
            for side in range(2):
                piece = rows[:, side * cols : (side + 1) * cols]
                gives[side][x // 2, y] = piece.astype(jnp.bfloat16)

    block = RING * part
    sources = ((near_ref, 0), (near_ref, block), (total, 0), (near_ref, 2 * block))
    in_place(core, spot_ref[1], spot_ref[2], -1, -1, sources, put)


def back(spot, far, weight, near):
    low, high = far
    part = low.shape[2]
    feats = weight.shape[2]
    shape = (2, RING, part, feats // 2)
    whole = pl.BlockSpec(memory_space=pltpu.VMEM)
    parts = pl.pallas_call(
        back_kernel,
        in_specs=[pl.BlockSpec(memory_space=pltpu.SMEM)] + [whole] * 4,
        out_specs=[whole] * 4,
        out_shape=[jax.ShapeDtypeStruct(shape, jnp.float32)] * 2
        + [jax.ShapeDtypeStruct(shape, jnp.bfloat16)] * 2,
        scratch_shapes=[pltpu.VMEM((RING * part, feats), jnp.float32)],
        compiler_params=pltpu.CompilerParams(vmem_limit_bytes=GRANT),
        name="back",
    )(spot, low, high, weight, near)
    parts = [part.reshape(-1, feats // 2) for part in parts]
    return parts[:2], parts[2:]


def outer_kernel(spot_ref, mine_ref, other_ref, *refs):
    around, before, low, high, after, out_ref, bias_ref, held = refs
    core = spot_ref[0]
    width = held.shape[-1]
    cut = low.shape[0]

    def put(x, y, piece, k):
        if piece is None:
            held[x // 2, lax.rem(x, 2), y] = low[k, 0] if k < cut else high[k - cut, 0]
        else:
            held[x // 2, lax.rem(x, 2), y] = piece[k, 0]

    in_place(core, spot_ref[1], spot_ref[2], -1, -1, (around, before, None, after), put)
    total = dot(held[:, core].reshape(-1, width), mine_ref[...], 0, 0)
    total += dot(held[:, 1 - core].reshape(-1, width), other_ref[...], 0, 0)
    out_ref[0] = total.astype(jnp.bfloat16)

    @pl.when(pl.program_id(0) == spot_ref[3])
    def _():
        grad = held[...].reshape(-1, width).astype(jnp.float32)
        bias_ref[...] = jnp.sum(grad, axis=0, keepdims=True)


def outer(spot, mine, other, pieces):
    _, nlayer, part, width = pieces[0].shape
    few, feats = mine.shape
    return pl.pallas_call(
        outer_kernel,
        grid_spec=pltpu.PrefetchScalarGridSpec(
            num_scalar_prefetch=1,
            grid=(nlayer,),
            in_specs=[
                pl.BlockSpec((few, feats), lambda m, _: (0, 0)),
                pl.BlockSpec((few, feats), lambda m, _: (0, 0)),
            ]
            + [
                pl.BlockSpec((piece.shape[0], 1, part, width), lambda m, _: (0, m, 0, 0))
                for piece in pieces
            ],
            out_specs=[
                pl.BlockSpec((1, width, feats), lambda m, _: (m, 0, 0)),
                pl.BlockSpec((1, width), lambda m, _: (0, 0)),
            ],
            scratch_shapes=[pltpu.VMEM((2, 2, RING, part, width), jnp.bfloat16)],
        ),
        out_shape=[
            jax.ShapeDtypeStruct((nlayer, width, feats), jnp.bfloat16),
            jax.ShapeDtypeStruct((1, width), jnp.float32),
        ],
        compiler_params=pltpu.CompilerParams(vmem_limit_bytes=GRANT),
        cost_estimate=pl.CostEstimate(
            flops=4 * nlayer * few * feats * width,
            transcendentals=0,
            bytes_accessed=2 * nlayer * feats * width,
        ),
        name="outer",
    )(spot, mine, other, *pieces)


def last_kernel(moved_ref, next_ref, mine_ref, other_ref, *refs):
    out_ref, bias_ref = refs[-2:]
    mine, other = mine_ref[...], other_ref[...]
    total = dot(moved_ref[...], mine, 1, 0) + dot(next_ref[...], other, 1, 0)
    out_ref[...] = total.astype(jnp.bfloat16)
    sums = [jnp.sum(g.astype(jnp.float32), axis=0, keepdims=True) for g in (mine, other)]
    bias_ref[...] = sums[0] + sums[1]


def last(side, moved, moved_next, mine, other, before):
    width, few = moved.shape
    cols = mine.shape[1]
    cut = min(cols, 256)
    first = side * (cols // cut)
    return pl.pallas_call(
        last_kernel,
        grid=(cols // cut,),
        in_specs=[
            pl.BlockSpec((width, few), lambda n: (0, 0)),
            pl.BlockSpec((width, few), lambda n: (0, 0)),
            pl.BlockSpec((few, cut), lambda n: (0, n)),
            pl.BlockSpec((few, cut), lambda n: (0, n)),
        ]
        + [pl.BlockSpec(memory_space=pl.ANY)] * len(before),
        out_specs=[
            pl.BlockSpec((width, cut), lambda n: (0, first + n)),
            pl.BlockSpec((1, cut), lambda n: (0, first + n)),
        ],
        out_shape=[
            jax.ShapeDtypeStruct((width, 2 * cols), jnp.bfloat16),
            jax.ShapeDtypeStruct((1, 2 * cols), jnp.float32),
        ],
        input_output_aliases={4 + k: k for k in range(len(before))},
        compiler_params=pltpu.CompilerParams(vmem_limit_bytes=GRANT),
    )(moved, moved_next, mine, other, *before)


def step(captured, target, enc_weight, enc_bias, dec_weight, dec_bias):
    layer = lax.axis_index("layer")
    half = lax.axis_index("half")
    core = lax.axis_index("core")
    nlayer = dec_weight.shape[1]
    width = enc_weight.shape[1]
    feats = enc_weight.shape[2]
    rows = captured.shape[1]
    tokens = rows * lax.axis_size(TOK)
    x, y = lax.axis_index("x"), lax.axis_index("y")
    first = jnp.where(core == 0, x, y)
    second = jnp.where(core == 0, y, x)
    spot = jnp.stack([core, first, second, layer, half])
    scale = 1.0 / math.sqrt(tokens)
    encoder = enc_weight[0]
    decoder = dec_weight[0].swapaxes(1, 2)

    cols = feats // 2
    theirs = lax.dynamic_slice_in_dim(encoder, (1 - half) * cols, cols, 1)
    theirs, captured, spot = lax.optimization_barrier((theirs, captured, spot))
    crossed = swapped(theirs, "half")
    small = captured[0].T
    small = both(small, swapped(small, "half"), half, 1)
    encoder, small = lax.optimization_barrier((encoder, small))
    mine = lax.dynamic_slice_in_dim(encoder, half * cols, cols, 1)
    mine_next = swapped(mine, "core")
    pieces = gathered(small)
    wide, moved, give = widths(spot, pieces)
    give, crossed = lax.optimization_barrier((give, crossed))
    crossed_next = swapped(crossed, "core")
    moved_next = swapped(give.reshape(width, -1), "core")
    crossed_next, moved_next = lax.optimization_barrier((crossed_next, moved_next))
    moved = moved.reshape(width, -1)
    act = encode(
        spot,
        wide.reshape(RING, width, -1),
        enc_bias.reshape(2, 1, cols),
        (mine, mine_next, crossed, crossed_next),
    )
    act = both(act, swapped(act, "half"), half, 1)
    act_next = swapped(act, "core")

    held = decoder
    taken = [None] * RING
    for steps in ((2,), (1, 3), (0,)):
        sums = decode(steps, spot, act, act_next, held, target.shape[1])
        for j, part in zip(steps, sums):
            taken[j] = turned(part, j, True) if j else part
    parts = halfway(spot, dec_bias, target[0], taken)
    recon = parts[0]
    for k in range(1, RING):
        recon = recon + turned(parts[k], k, False).astype(jnp.float32)
    writes = lax.broadcasted_iota(jnp.int32, (nlayer, 1, 1), 0)
    recon = jnp.where(writes >= layer, recon, 0.0)
    shared = recon.astype(jnp.bfloat16)
    for far in range(1, nlayer):
        least = min(max(k, (k + far) % nlayer) for k in range(nlayer))
        ring = [(k, (k + far) % nlayer) for k in range(nlayer)]
        taken = lax.ppermute(shared[least:], "layer", ring).astype(jnp.float32)
        recon = recon + jnp.pad(taken, ((least, 0), (0, 0), (0, 0)))
    scaled = jnp.where(writes >= layer, recon * scale, 0.0)
    around, before, far, after = forwarded(scaled.astype(jnp.bfloat16))

    near = near_rows((around, before, after), held)
    keeps, gives = back(spot, far, held, near)
    crossings = []
    for side in range(2):
        keep = keeps[side] + swapped(gives[side], "core").astype(jnp.float32)
        keeps[side] = lax.optimization_barrier(keep.astype(jnp.bfloat16))
        crossings.append(swapped(keeps[side], "half"))
    grads, _ = lax.optimization_barrier(((around, before, *far, after), keeps))
    dec_grads, dec_bias_grad = outer(spot, act, act_next, grads)
    results = ()
    for side in range(2):
        grad_mine = keeps[side].astype(jnp.float32) + crossings[side].astype(jnp.float32)
        on = act[:, side * cols : (side + 1) * cols] > 0
        grad_pre = jnp.where(on, grad_mine, 0.0).astype(jnp.bfloat16)
        other = swapped(grad_pre, "core")
        results = last(side, moved, moved_next, grad_pre, other, results)
    enc_grad, enc_bias_grad = results
    return (enc_grad[None], enc_bias_grad, dec_grads.swapaxes(1, 2)[None], dec_bias_grad)


def solution(mesh):
    split = Mesh(
        mesh.devices.reshape(4, 4, mesh.shape["layer"], 2, 2),
        ("x", "y", "layer", "half", "core"),
    )
    return jax.shard_map(
        step,
        mesh=split,
        in_specs=(
            P("layer", TOK, FEAT),
            P("layer", FEAT, TOK),
            P("layer", TOK, FEAT),
            P("layer", FEAT),
            P("layer", None, FEAT, TOK),
            P("layer", TOK),
        ),
        out_specs=(
            P("layer", TOK, FEAT),
            P("layer", FEAT),
            P("layer", None, FEAT, TOK),
            P("layer", TOK),
        ),
        check_vma=False,
    )
```
